32 devices in a mesh: dp: 8 (over z, y), expert: 4 (over x, core).
Axes of the slice: x: 2, y: 2, z: 4, core: 2. Of those that a mesh axis runs over, the one named last changes fastest.
Arguments:
- residual: bfloat16 [4096, 3072], P(('dp', 'expert')), may hold values from -36 to 36
- context: bfloat16 [4096, 24, 128], P('dp', 'expert'), may hold values from -6 to 6
- master: float32 [24, 128, 3072], P('expert', 'dp'), may hold values from -0.109375 to 0.109375
- grad: float32 [24, 128, 3072], P('expert', 'dp'), may hold values from -6 to 6
- moment: float32 [24, 128, 3072], P('expert', 'dp'), may hold values from -1.8 to 1.8
- second: float32 [24, 128, 3072], P('expert', 'dp'), may hold values from 0.0005 to 0.02
- gain: float32 [3072], replicated, may hold values from 0.5 to 1.5
- token_ids: int32 [4096], P(('dp', 'expert')), may hold values from 0 to 51199
- table_one: int32 [51200], replicated, may hold values from 0 to 7
- table_two: int32 [51200], replicated, may hold values from 0 to 7
- w_in: bfloat16 [8, 1536, 5120], P('dp', None, 'expert'), may hold values from -0.15625 to 0.15625
- w_out: bfloat16 [8, 5120, 1536], P('dp', 'expert'), may hold values from -0.078125 to 0.078125
Outputs:
- mixed: bfloat16 [4096, 3072], P(('dp', 'expert'))
The draws below stay inside these ranges and needn't reach their ends.
All inputs are finite; a program needn't handle non-finite values.
Results may differ from the reference program's by a relative error of at most 0.009.
Values may be sent and summed in bfloat16 or wider, within the bound.
A program may use at most 64 MiB of HBM per device.

```python
import math
import jax
import jax.numpy as jnp
import numpy as np
from jax import lax

D = 3072
DH = 1536
FF = 5120
HEADS = 24
HDIM = 128
VOCAB = 51200
TOK_DEV = 128
TOKENS = 4096
EXPERTS = 8
CAP = 20
N_EXPERT = 4


def draw_residual(key, part):
    value_key, row_key, column_key = jax.random.split(jax.random.fold_in(key, 17), 3)
    values = jax.random.truncated_normal(value_key, -4.0, 4.0, (TOKENS, D), jnp.float32)
    row_scale = jnp.exp(jax.random.uniform(row_key, (TOKENS, 1), jnp.float32, jnp.log(0.3), jnp.log(3.0)))
    column_scale = jnp.exp(jax.random.uniform(column_key, (1, D), jnp.float32, jnp.log(0.3), jnp.log(3.0)))
    return (values * row_scale * column_scale).astype(jnp.bfloat16)


def touch_ends(result, key, least, top_value):
    longest = result.shape.index(max(result.shape))
    spots = []
    for shift in (0, 1):
        where = [jax.random.randint(jax.random.fold_in(key, axis), (), 0, length) for axis, length in enumerate(result.shape)]
        where[longest] = (where[longest] + shift) % result.shape[longest]
        spots.append(tuple(where))
    return result.at[spots[0]].set(least).at[spots[1]].set(top_value)


def levels(rng, extent, cuts, low, largest):
    factor_of = 1.0
    for dim, parts in cuts:
        steps = jax.random.uniform(jax.random.fold_in(jax.random.fold_in(rng, 6), dim), (parts,), jnp.float32, low / len(cuts), largest / len(cuts))
        factor_of = factor_of * jnp.repeat(jnp.exp(steps), extent[dim] // parts).reshape((-1,) + (1,) * (len(extent) - 1 - dim))
    return factor_of


def rank_bounds(number_of, skew):
    portions = [(1 << 20) // math.isqrt(grade ** skew) + 1 for grade in range(1, number_of + 1)]
    scale = 1 + sum(portions) // (1 << 30)
    return np.cumsum(np.array([max(1, weight // scale) for weight in portions]))


def ranked_ids(key, extent, number_of, lean):
    grid = rank_bounds(number_of, lean)
    ticket = jax.random.randint(jax.random.fold_in(key, 1), extent, 0, int(grid[number_of - 1]))
    standing = jnp.searchsorted(jnp.asarray(grid, jnp.int32), ticket, side="right")
    return jax.random.permutation(jax.random.fold_in(key, 2), number_of)[standing].astype(jnp.int32)


def normal_values(key, shape, deviation, reach, cuts=(), held_as=jnp.bfloat16):
    drawn = jax.random.normal(key, shape, jnp.float32) * deviation
    if len(cuts) > 0:
        drawn = levels(key, shape, cuts, -0.22, 0.18) * drawn
    return jnp.clip(drawn, min=-reach, max=reach).astype(held_as)


def setup_inputs(seed: int = 0) -> dict:
    arg_keys = jax.random.split(jax.random.key(seed), 13)
    return {
        "residual": draw_residual(jax.random.fold_in(arg_keys[12], 71), 0),
        "context": normal_values(arg_keys[1], (TOKENS, HEADS, HDIM), 1.0, 6.0, ((0, 8), (1, 4))),
        "master": normal_values(arg_keys[2], (HEADS, HDIM, D), (HEADS * HDIM) ** -0.5, 0.109375, ((0, 4), (1, 8)), jnp.float32),
        "grad": normal_values(arg_keys[3], (HEADS, HDIM, D), 1.0, 6.0, ((0, 4), (1, 8)), jnp.float32),
        "moment": normal_values(arg_keys[4], (HEADS, HDIM, D), 0.3, 1.8, ((0, 4), (1, 8)), jnp.float32),
        "second": jnp.clip(jnp.exp(math.log(0.02) - 3.6888794 * jax.random.uniform(arg_keys[5], (HEADS, HDIM, D), jnp.float32) ** levels(arg_keys[5], (HEADS, HDIM, D), ((0, 4), (1, 8)), -0.2, 0.2)), 0.0005, 0.02),
        "gain": jnp.clip(1.0 + 0.1 * jax.random.normal(arg_keys[6], (D,), jnp.float32), 0.5, 1.5),
        "token_ids": touch_ends(ranked_ids(arg_keys[7], (TOKENS,), VOCAB, 2), jax.random.fold_in(arg_keys[7], 3), 0, VOCAB - 1).astype(jnp.int32),
        "table_one": touch_ends(jax.random.randint(arg_keys[8], (VOCAB,), 0, EXPERTS), jax.random.fold_in(arg_keys[8], 1), 0, EXPERTS - 1).astype(jnp.int32),
        "table_two": touch_ends(jax.random.randint(arg_keys[9], (VOCAB,), 0, EXPERTS), jax.random.fold_in(arg_keys[9], 1), 0, EXPERTS - 1).astype(jnp.int32),
        "w_in": normal_values(arg_keys[10], (EXPERTS, DH, FF), DH ** -0.5, 0.15625, ((0, 8), (2, 4))),
        "w_out": normal_values(arg_keys[11], (EXPERTS, FF, DH), FF ** -0.5, 0.078125, ((0, 8), (1, 4))),
    }


lr_rate = 0.01
beta_one = 0.9
beta_two = 0.999
adam_step = 10.0
eps_adam = 1e-08
eps_norm = 1e-05

def adam_weight(master, grad, moment, second):
    new_moment = beta_one * moment + (1.0 - beta_one) * grad
    new_second = beta_two * second + (1.0 - beta_two) * grad * grad
    corr_one = 1.0 - beta_one ** adam_step
    corr_two = 1.0 - beta_two ** adam_step
    update = new_moment / corr_one / (jnp.sqrt(new_second / corr_two) + eps_adam)
    return (master - lr_rate * update).astype(jnp.bfloat16)

def slot_tables(routes_of, experts, capacity):
    onehot = (routes_of[..., None] == jnp.arange(experts, dtype=jnp.int32)).astype(jnp.int32)
    before = jnp.cumsum(onehot, axis=-2) - onehot
    slot_rank = lax.optimization_barrier(jnp.sum(before * onehot, axis=-1))
    match_expert = routes_of[..., None, :] == jnp.arange(experts, dtype=jnp.int32)[:, None]
    match_slot = slot_rank[..., None, :] == jnp.arange(capacity, dtype=jnp.int32)[:, None]
    return (match_expert[..., :, None, :] & match_slot[..., None, :, :]).astype(jnp.bfloat16)

def reference(residual, context, master, grad, moment, second, gain, token_ids, table_one, table_two, w_in, w_out):
    weight = adam_weight(master, grad, moment, second)
    group_width = HEADS // N_EXPERT * HDIM
    ctx_groups = jnp.transpose(context.reshape(TOKENS, N_EXPERT, group_width), (1, 0, 2))
    weight_groups = weight.reshape(N_EXPERT, group_width, D)

    def add_group(running, inputs):
        term = jnp.dot(inputs[0], inputs[1], preferred_element_type=jnp.float32).astype(jnp.bfloat16)
        term = lax.optimization_barrier(term)
        return (running + term.astype(jnp.float32), None)
    attn, _ = lax.scan(add_group, jnp.zeros((TOKENS, D), jnp.float32), (ctx_groups, weight_groups))
    state = residual.astype(jnp.float32) + attn
    scale = lax.rsqrt(lax.optimization_barrier(jnp.mean(state * state, axis=-1, keepdims=True)) + eps_norm)
    normed = (state * scale * gain.astype(jnp.float32)).astype(jnp.bfloat16)
    blocks = TOKENS // TOK_DEV
    halves_wide = normed.reshape(blocks, TOK_DEV, 2, DH).astype(jnp.float32)
    routes = jnp.stack([table_one[token_ids], table_two[token_ids]]).reshape(2, blocks, TOK_DEV)
    dispatch = slot_tables(routes, EXPERTS, CAP)
    by_expert = jnp.transpose(dispatch, (2, 0, 1, 3, 4)).astype(jnp.float32)
    slice_width = FF // N_EXPERT

    def one_expert(running, inputs):
        table, weight_in, weight_out = inputs
        gathered = jnp.einsum('kbst,btkd->kbsd', table, halves_wide)
        rows_in = gathered.astype(jnp.bfloat16).reshape(-1, DH)
        inner = jnp.dot(rows_in, weight_in, preferred_element_type=jnp.float32)
        hidden = jax.nn.gelu(inner, approximate=True).astype(jnp.bfloat16)
        hidden_parts = hidden.reshape(-1, N_EXPERT, slice_width).astype(jnp.float32)
        out_parts = weight_out.reshape(N_EXPERT, slice_width, DH).astype(jnp.float32)
        pieces = jnp.einsum('rcf,cfd->crd', hidden_parts, out_parts).astype(jnp.bfloat16)
        pieces = lax.optimization_barrier(pieces)
        expert_out = lax.optimization_barrier(jnp.sum(pieces.astype(jnp.float32), axis=0)).astype(jnp.bfloat16)
        expert_out = lax.optimization_barrier(expert_out)
        expert_out = expert_out.astype(jnp.float32).reshape(2, blocks, CAP, DH)
        return (running + jnp.einsum('kbst,kbsd->btkd', table, expert_out), None)
    routed, _ = lax.scan(one_expert, jnp.zeros((blocks, TOK_DEV, 2, DH), jnp.float32), (by_expert, w_in, w_out))
    return (state + routed.reshape(TOKENS, D)).astype(jnp.bfloat16)
```

```python
import functools

import jax
import jax.numpy as jnp
from jax import lax
from jax.experimental import pallas as pl
from jax.experimental.pallas import tpu as pltpu
from jax.sharding import PartitionSpec as P

lr_rate = 0.01
beta_one = 0.9
beta_two = 0.999
adam_step = 10.0
eps_adam = 1e-08
eps_norm = 1e-05

MESH = pl.DeviceIdType.MESH


def adam_weight(master, grad, moment, second):
    new_moment = beta_one * moment + (1.0 - beta_one) * grad
    new_second = beta_two * second + (1.0 - beta_two) * grad * grad
    corr_one = 1.0 - beta_one**adam_step
    corr_two = 1.0 - beta_two**adam_step
    update = new_moment / corr_one / (jnp.sqrt(new_second / corr_two) + eps_adam)
    return (master - lr_rate * update).astype(jnp.bfloat16)


def slot_tables(routes_of, experts, capacity):
    onehot = (routes_of[..., None] == jnp.arange(experts, dtype=jnp.int32)).astype(jnp.int32)
    before = jnp.cumsum(onehot, axis=-2) - onehot
    slot_rank = jnp.sum(before * onehot, axis=-1)
    match_expert = routes_of[..., None, :] == jnp.arange(experts, dtype=jnp.int32)[:, None]
    match_slot = slot_rank[..., None, :] == jnp.arange(capacity, dtype=jnp.int32)[:, None]
    return (match_expert[..., :, None, :] & match_slot[..., None, :, :]).astype(jnp.bfloat16)


def remote(src, dst, send_sem, recv_sem, where):
    return pltpu.make_async_remote_copy(
        src_ref=src, dst_ref=dst, send_sem=send_sem, recv_sem=recv_sem,
        device_id=where, device_id_type=MESH,
    )


def greet(partners):
    barrier = pltpu.get_barrier_semaphore()
    for where in partners:
        pl.semaphore_signal(barrier, inc=1, device_id=where, device_id_type=MESH)
    pl.semaphore_wait(barrier, len(partners))


def proj_kernel(
    n, width, exp_size, chunk,
    master, grad, moment, second, ctx, resid, gain,
    state, normed,
    wbuf, own, snd, prec, xsnd, xrec,
    sz, rz, sy, ry, sp, rp, sx, rx,
):
    chunks = width // chunk
    far, chips = n // 2, exp_size // 2
    heads, _, rows = wbuf.shape[1:4]
    tok = resid.shape[0]
    d, e = lax.axis_index("dp"), lax.axis_index("expert")
    a, b, x, c = d // 2, d % 2, e // 2, e % 2
    mate = (d, x * 2 + 1 - c)
    pair = (a * 2 + 1 - b, e)

    def z_dev(j):
        return (((a + j) % far) * 2 + b, e)

    def x_dev(j):
        return (d, ((x + j) % chips) * 2 + c)

    greet([z_dev(j) for j in range(1, far)] + [pair, mate] + [x_dev(j) for j in range(1, chips)])

    def z_copy(t, j, whose):
        spot = wbuf.at[t, :, whose]
        return remote(spot, spot, sz.at[t, j - 1], rz.at[t, j - 1], z_dev(j))

    def y_copy(t, j, whose):
        spot = wbuf.at[t, :, whose]
        return remote(spot, spot, sy.at[t, j], ry.at[t, j], pair)

    def mate_copy(t, xx):
        return remote(snd.at[t, xx], prec.at[t, xx], sp.at[t, xx], rp.at[t, xx], mate)

    def x_copy(t, j, there):
        return remote(xsnd.at[t, (x + j) % chips], xrec.at[t, there], sx.at[t, j - 1], rx.at[t, j - 1], x_dev(j))

    def cols(t):
        return pl.ds(pl.multiple_of(t * chunk, chunk), chunk)

    def stage_send(t):
        k = cols(t)
        wbuf[t, :, d] = adam_weight(master[:, :, k], grad[:, :, k], moment[:, :, k], second[:, :, k])
        for j in range(far - 1, 0, -1):
            z_copy(t, j, d).start()
        y_copy(t, 0, d).start()

    def stage_forward(t):
        for j in range(1, far):
            whose = ((a - j + far) % far) * 2 + b
            z_copy(t, j, whose).wait_recv()
            y_copy(t, j, whose).start()

    def stage_dot(t):
        for j in range(far):
            y_copy(t, j, ((a - j + far) % far) * 2 + 1 - b).wait_recv()
        for side in (1, 0):
            for j in range(chips):
                xx = (x + j) % chips
                block = xx * 2 + (1 - c if side else c)
                lhs = ctx[pl.ds(pl.multiple_of(block * tok, tok), tok), :]
                w = wbuf[t].reshape(heads * n * rows, chunk)
                term = jnp.dot(lhs, w, preferred_element_type=jnp.float32).astype(jnp.bfloat16)
                if side:
                    snd[t, xx] = term
                    mate_copy(t, xx).start()
                else:
                    own[t, xx] = term

    def stage_pair(t):
        for j in range(chips):
            mate_copy(t, (x + j) % chips).wait_recv()
        for j in range(1, chips):
            xx = (x + j) % chips
            both = own[t, xx].astype(jnp.float32) + prec[t, xx].astype(jnp.float32)
            xsnd[t, xx] = both.astype(jnp.bfloat16)
            x_copy(t, j, x).start()

    def stage_state(t):
        total = own[t, x].astype(jnp.float32) + prec[t, x].astype(jnp.float32)
        for j in range(1, chips):
            there = (x - j + chips) % chips
            x_copy(t, j, there).wait_recv()
            total = total + xrec[t, there].astype(jnp.float32)
        state[:, cols(t)] = resid[:, cols(t)].astype(jnp.float32) + total

    def step(t, carry):
        for lag, stage in ((0, stage_send), (2, stage_forward), (3, stage_dot), (4, stage_pair), (5, stage_state)):
            @pl.when((t >= lag) & (t < lag + chunks))
            def _():
                stage(t - lag)
        return carry

    lax.fori_loop(0, chunks + 5, step, 0)
    whole = state[...]
    scale = lax.rsqrt(jnp.mean(whole * whole, axis=-1, keepdims=True) + eps_norm)
    normed[...] = (whole * scale * gain[...]).astype(jnp.bfloat16)

    def drain(t, carry):
        for j in range(1, far):
            z_copy(t, j, d).wait_send()
        for j in range(far):
            y_copy(t, j, ((a - j + far) % far) * 2 + b).wait_send()
        for j in range(chips):
            mate_copy(t, (x + j) % chips).wait_send()
        for j in range(1, chips):
            x_copy(t, j, x).wait_send()
        return carry

    lax.fori_loop(0, chunks, drain, 0)


def project(n, exp_size, context, residual, master, grad, moment, second, gain):
    tok, width = residual.shape
    chunk = min(512, width)
    chunks = width // chunk
    heads, rows = master.shape[:2]
    far, chips = n // 2, exp_size // 2
    dma = pltpu.SemaphoreType.DMA
    vmem = pl.BlockSpec(memory_space=pltpu.VMEM)
    term = pltpu.VMEM((chunks, chips, tok, chunk), jnp.bfloat16)
    return pl.pallas_call(
        functools.partial(proj_kernel, n, width, exp_size, chunk),
        out_shape=(
            jax.ShapeDtypeStruct((tok, width), jnp.float32),
            jax.ShapeDtypeStruct((tok, width), jnp.bfloat16),
        ),
        in_specs=[vmem] * 7,
        out_specs=(vmem, vmem),
        scratch_shapes=[
            pltpu.VMEM((chunks, heads, n, rows, chunk), jnp.bfloat16),
            term, term, term, term, term,
            dma((chunks, far - 1)), dma((chunks, far - 1)),
            dma((chunks, far)), dma((chunks, far)),
            dma((chunks, chips)), dma((chunks, chips)),
            dma((chunks, chips - 1)), dma((chunks, chips - 1)),
        ],
        compiler_params=pltpu.CompilerParams(collective_id=0, has_side_effects=True),
        name="project",
    )(master, grad, moment, second, context.reshape(context.shape[0], -1), residual, gain.reshape(1, -1))


def moe_kernel(
    n, exp_size,
    normed, state, pick, place, w_in, w_out,
    mixed,
    outg, rows, part, prec, xsnd, xrec, acc, fin, ret,
    s1, r1, sm, rm, sx, rx, sp, rp, sy, ry, sb, rb,
):
    chips = exp_size // 2
    slots, half = outg.shape[1:]
    tok = normed.shape[0]
    d, e = lax.axis_index("dp"), lax.axis_index("expert")
    x, c = e // 2, e % 2
    mate = (d, x * 2 + 1 - c)

    def x_dev(j):
        return (d, ((x + j) % chips) * 2 + c)

    greet([((d + k) % n, e) for k in range(1, n)] + [mate] + [x_dev(j) for j in range(1, chips)])

    def out_copy(k, whose):
        return remote(outg.at[(d + k) % n], rows.at[whose, e], s1.at[k], r1.at[k], ((d + k) % n, e))

    def wide_copy(k, j, col):
        s = (d - k + n) % n
        return remote(rows.at[s, e], rows.at[s, col], sx.at[k, j - 1], rx.at[k, j - 1], x_dev(j))

    def mate_copy(k, j, core):
        spot = rows.at[(d - k + n) % n, ((x - j + chips) % chips) * 2 + core]
        return remote(spot, spot, sm.at[k, j], rm.at[k, j], mate)

    def part_copy(k, j):
        s, xx = (d - k + n) % n, (x + j) % chips
        return remote(part.at[s, xx * 2 + 1 - c], prec.at[s, xx], sp.at[k, j], rp.at[k, j], mate)

    def sum_copy(k, j, there):
        s = (d - k + n) % n
        return remote(xsnd.at[s, (x + j) % chips], xrec.at[s, there], sy.at[k, j - 1], ry.at[k, j - 1], x_dev(j))

    def back_copy(k, whose):
        s = (d - k + n) % n
        return remote(fin.at[s], ret.at[whose], sb.at[k], rb.at[k], (s, e))

    picked = jnp.dot(pick[:, :tok], normed[:, :half], preferred_element_type=jnp.float32)
    picked = picked + jnp.dot(pick[:, tok:], normed[:, half:], preferred_element_type=jnp.float32)
    outg[...] = picked.reshape(n, slots, half).astype(jnp.bfloat16)
    for k in range(1, n):
        out_copy(k, d).start()
    rows[d, e] = outg[d]

    def stage_forward(k):
        @pl.when(k > 0)
        def _():
            out_copy(k, (d - k + n) % n).wait_recv()
        for j in range(1, chips):
            wide_copy(k, j, e).start()
        mate_copy(k, 0, c).start()

    def stage_mate(k):
        for j in range(1, chips):
            wide_copy(k, j, ((x - j + chips) % chips) * 2 + c).wait_recv()
            mate_copy(k, j, c).start()

    def stage_dot(k):
        s = (d - k + n) % n
        for j in range(chips):
            mate_copy(k, j, 1 - c).wait_recv()
        block = rows[s].astype(jnp.float32).reshape(exp_size * slots, half).astype(jnp.bfloat16)
        inner = jnp.dot(block, w_in[...], preferred_element_type=jnp.float32)
        hidden = jax.nn.gelu(inner, approximate=True).astype(jnp.bfloat16)
        piece = jnp.dot(hidden, w_out[...], preferred_element_type=jnp.float32)
        part[s] = piece.reshape(exp_size, slots, half).astype(jnp.bfloat16)
        for j in range(chips):
            part_copy(k, j).start()

    def stage_pair(k):
        s = (d - k + n) % n
        for j in range(chips):
            part_copy(k, j).wait_recv()
        for j in range(chips):
            xx = (x + j) % chips
            both = part[s, xx * 2 + c].astype(jnp.float32) + prec[s, xx].astype(jnp.float32)
            if j:
                xsnd[s, xx] = both.astype(jnp.bfloat16)
                sum_copy(k, j, x).start()
            else:
                acc[s] = both

    def stage_back(k):
        s = (d - k + n) % n
        total = acc[s]
        for j in range(1, chips):
            there = (x - j + chips) % chips
            sum_copy(k, j, there).wait_recv()
            total = total + xrec[s, there].astype(jnp.float32)

        @pl.when(k > 0)
        def _():
            fin[s] = total.astype(jnp.bfloat16)
            back_copy(k, d).start()

        @pl.when(k == 0)
        def _():
            ret[d] = total.astype(jnp.bfloat16)

    def step(t, carry):
        for lag, stage in ((0, stage_forward), (1, stage_mate), (2, stage_dot), (3, stage_pair), (4, stage_back)):
            @pl.when((t >= lag) & (t < lag + n))
            def _():
                stage(t - lag)
        return carry

    lax.fori_loop(0, n + 4, step, 0)
    for k in range(1, n):
        back_copy(k, (d + k) % n).wait_recv()
    back = ret[...].astype(jnp.float32).reshape(n * slots, half).astype(jnp.bfloat16)
    for k in range(2):
        routed = jnp.dot(place[pl.ds(k * tok, tok), :], back, preferred_element_type=jnp.float32)
        mixed[:, pl.ds(k * half, half)] = (state[:, pl.ds(k * half, half)] + routed).astype(jnp.bfloat16)

    def drain(k, carry):
        @pl.when(k > 0)
        def _():
            out_copy(k, d).wait_send()
            back_copy(k, d).wait_send()
        for j in range(chips):
            mate_copy(k, j, c).wait_send()
            part_copy(k, j).wait_send()
        for j in range(1, chips):
            wide_copy(k, j, e).wait_send()
            sum_copy(k, j, x).wait_send()
        return carry

    lax.fori_loop(0, n, drain, 0)


def mix_experts(n, exp_size, capacity, state, normed, routes, w_in, w_out):
    tok, width = state.shape
    half, slots, chips = width // 2, 2 * capacity, exp_size // 2
    dispatch = slot_tables(routes, n, capacity)
    blank = jnp.zeros_like(dispatch[0])
    pick = jnp.stack(
        [jnp.concatenate([dispatch[0], blank], -1), jnp.concatenate([blank, dispatch[1]], -1)], axis=1
    ).reshape(n * slots, 2 * tok)
    dma = pltpu.SemaphoreType.DMA
    vmem = pl.BlockSpec(memory_space=pltpu.VMEM)
    bf = jnp.bfloat16
    pairs = pltpu.VMEM((n, chips, slots, half), bf)
    full = pltpu.VMEM((n, exp_size, slots, half), bf)
    one = pltpu.VMEM((n, slots, half), bf)
    return pl.pallas_call(
        functools.partial(moe_kernel, n, exp_size),
        out_shape=jax.ShapeDtypeStruct((tok, width), bf),
        in_specs=[vmem] * 6,
        out_specs=vmem,
        scratch_shapes=[
            one, full, full, pairs, pairs, pairs,
            pltpu.VMEM((n, slots, half), jnp.float32), one, one,
            dma((n,)), dma((n,)),
            dma((n, chips)), dma((n, chips)),
            dma((n, chips - 1)), dma((n, chips - 1)),
            dma((n, chips)), dma((n, chips)),
            dma((n, chips - 1)), dma((n, chips - 1)),
            dma((n,)), dma((n,)),
        ],
        compiler_params=pltpu.CompilerParams(collective_id=1, has_side_effects=True),
        name="mix_experts",
    )(normed, state, pick, pick.T, w_in[0], w_out[0])


def plain_project(context, residual, master, grad, moment, second, gain):
    model_width = residual.shape[1]
    fresh = adam_weight(master, grad, moment, second)
    weight_all = lax.all_gather(fresh, "dp", axis=1, tiled=True)
    weight_rows = weight_all.reshape(-1, model_width)
    ctx_rows = context.reshape(context.shape[0], -1)
    attn = lax.psum_scatter(
        jnp.dot(ctx_rows, weight_rows, preferred_element_type=jnp.float32).astype(jnp.bfloat16),
        "expert",
        scatter_dimension=0,
        tiled=True,
    ).astype(jnp.float32)
    state = residual.astype(jnp.float32) + attn
    scale = lax.rsqrt(jnp.mean(state * state, axis=-1, keepdims=True) + eps_norm)
    return state, (state * scale * gain).astype(jnp.bfloat16)


def plain_mix(experts, capacity, state, normed, routes, w_in, w_out):
    tok_count, model_width = state.shape
    half_width = model_width // 2
    halves = normed.reshape(tok_count, 2, half_width)
    dispatch = slot_tables(routes, experts, capacity)
    outgoing = jnp.einsum(
        "kest,tkd->eksd", dispatch, halves, preferred_element_type=jnp.float32
    ).astype(jnp.bfloat16)
    arrived = lax.all_to_all(outgoing, "dp", split_axis=0, concat_axis=0, tiled=True)
    rows_here = arrived.reshape(-1, half_width)
    inner = jnp.dot(
        lax.all_gather(rows_here, "expert", axis=0, tiled=True),
        w_in[0],
        preferred_element_type=jnp.float32,
    )
    hidden = jax.nn.gelu(inner, approximate=True).astype(jnp.bfloat16)
    partial_rows = jnp.dot(hidden, w_out[0], preferred_element_type=jnp.float32)
    expert_out = lax.psum_scatter(
        partial_rows.astype(jnp.bfloat16), "expert", scatter_dimension=0, tiled=True
    )
    shaped = expert_out.reshape(experts, 2, capacity, half_width)
    returned = lax.all_to_all(shaped, "dp", split_axis=0, concat_axis=0, tiled=True)
    routed = jnp.einsum("kest,eksd->tkd", dispatch, returned, preferred_element_type=jnp.float32)
    return (state + routed.reshape(tok_count, model_width)).astype(jnp.bfloat16)


def on_device(
    n, exp_size,
    residual, context, master, grad, moment, second, gain, token_ids, table_one, table_two, w_in, w_out,
):
    experts = n * w_in.shape[0]
    tok_count = residual.shape[0]
    capacity = max(2, 5 * tok_count // (4 * experts))
    even = n % 2 == 0 and exp_size % 2 == 0 and n > 2 and exp_size > 2
    routes = jnp.stack([table_one[token_ids], table_two[token_ids]])
    if even and master.shape[1] % 16 == 0 and tok_count % 128 == 0 and residual.shape[1] % 512 == 0:
        state, normed = project(n, exp_size, context, residual, master, grad, moment, second, gain)
    else:
        state, normed = plain_project(context, residual, master, grad, moment, second, gain)
    if even and (2 * capacity) % 8 == 0 and w_in.shape[0] == 1 and tok_count % 128 == 0:
        return mix_experts(n, exp_size, capacity, state, normed, routes, w_in, w_out)
    return plain_mix(experts, capacity, state, normed, routes, w_in, w_out)


def solution(mesh):
    return jax.shard_map(
        functools.partial(on_device, mesh.shape["dp"], mesh.shape["expert"]),
        mesh=mesh,
        in_specs=(
            P(("dp", "expert"), None),
            P("dp", "expert", None),
            P("expert", "dp", None),
            P("expert", "dp", None),
            P("expert", "dp", None),
            P("expert", "dp", None),
            P(),
            P(("dp", "expert")),
            P(),
            P(),
            P("dp", None, "expert"),
            P("dp", "expert", None),
        ),
        out_specs=P(("dp", "expert"), None),
        check_vma=False,
    )
```
